512 devices in a mesh: dp: 4 (over x), expert: 128 (over z, y, core).
Axes of the slice: x: 4, y: 8, z: 8, core: 2. Of those that a mesh axis runs over, the one named last changes fastest.
Arguments:
- x_rows: bfloat16 [65536, 1024], P(('dp', 'expert')), may hold values from -6 to 6
- expert_ids: int32 [65536, 1], P(('dp', 'expert')), may hold values from 0 to 127; in each aligned block of 128 rows (0 to 127, 128 to 255, ...) at most 2 rows name the same one
- gates: float32 [65536, 1], P(('dp', 'expert')), may hold values from 0.1 to 1
- cotangent: bfloat16 [65536, 1024], P(('dp', 'expert')), may hold values from -6 to 6
- w_gate: bfloat16 [128, 1024, 384], P('expert', 'dp'), may hold values from -0.1875 to 0.1875
- w_up: bfloat16 [128, 1024, 384], P('expert', 'dp'), may hold values from -0.1875 to 0.1875
- w_down: bfloat16 [128, 384, 1024], P('expert', None, 'dp'), may hold values from -0.3125 to 0.3125
Outputs:
- gated_out: bfloat16 [65536, 1024], P(('dp', 'expert'))
- input_grad: bfloat16 [65536, 1024], P(('dp', 'expert'))
- gate_grad: float32 [65536, 1], P(('dp', 'expert'))
- grad_gate: bfloat16 [128, 1024, 384], P('expert', 'dp')
- grad_up: bfloat16 [128, 1024, 384], P('expert', 'dp')
- grad_down: bfloat16 [128, 384, 1024], P('expert', None, 'dp')
The draws below stay inside these ranges and needn't reach their ends.
Inputs may be any that keep to these rules, and one draw needn't show every extreme that they name: `expert_ids`: among the rows of one device each expert id occurs at most 2 times, and in some device's rows some expert occurs exactly 2 times.
All inputs are finite; a program needn't handle non-finite values.
Results may differ from the reference program's by a relative error of at most 0.009.
Values may be sent and summed in bfloat16 or wider, within the bound.
No kernel may reach another device: no remote copies, remote signals or barrier semaphores. Data moves between devices by JAX's collectives and lax.ppermute only.
A program may use at most 64 MiB of HBM per device.

```python
import math
import jax
import jax.numpy as jnp
import numpy as np
from jax import lax

D = 1024
HID = 384
ROWS_DEV = 128
EXPERTS = 128
CAP = 2
ROWS = 65536
N_DP = 4
N_EXPERT = 128


def steps_of(stream_key, dims, cuts, smallest, high):
    factor_of, own = 1.0, jax.random.fold_in(stream_key, 6)
    for dim, parts in cuts:
        heights = jnp.exp(jax.random.uniform(jax.random.fold_in(own, dim), (parts,), jnp.float32, smallest / len(cuts), high / len(cuts)))
        factor_of = factor_of * jnp.repeat(heights, dims[dim] // parts).reshape([-1 if axis == dim else 1 for axis in range(len(dims))])
    return factor_of


def assign_block(key, own, number, rows, count, top, most, slope):
    order = jax.random.permutation(key, count)
    crowded, common = shares(count, rows * top, most, slope, True), shares(count, rows * top, most, slope, False)
    places = jnp.arange(count)

    def named(lengths, turn):
        used = int((lengths > 0).sum())
        fixed = max(1, used // 4)
        shifted = fixed + (places - fixed + turn * (used - fixed)) % max(1, count - fixed)
        return jnp.zeros((count,), jnp.int32).at[order[jnp.where(places < fixed, places, shifted)]].set(jnp.asarray(lengths, jnp.int32))

    lengths = jnp.where(number % 4 == 0, named(crowded, number // 4), named(common, number - number // 4 - 1))
    mixed = jax.random.permutation(jax.random.fold_in(own, 3), count)
    donor, receiver = mixed[0:count // 2 * 2:2], mixed[1:count // 2 * 2:2]
    room = jnp.minimum(lengths[donor] - 1, most - lengths[receiver]) // 2
    room = jnp.where((donor == order[0]) | (receiver == order[0]) | (lengths[receiver] == 0), 0, jnp.maximum(room, 0))
    shifted = jax.random.randint(jax.random.fold_in(own, 4), (count // 2,), 0, 1 << 20) % (room + 1)
    lengths = lengths.at[donor].add(-shifted).at[receiver].add(shifted)
    items = jnp.searchsorted(jnp.cumsum(lengths), jnp.arange(rows * top), side="right").astype(jnp.int32)
    listing = items.reshape(top, rows).T
    listing = listing[jax.random.permutation(jax.random.fold_in(own, 1), rows)]
    turn = jax.random.randint(jax.random.fold_in(own, 2), (rows, 1), 0, top)
    return jnp.take_along_axis(listing, (jnp.arange(top)[None, :] + turn) % top, axis=1)


def shares(amount, total, most, slope, full):
    loads = [(1 << 20) // math.isqrt(standing ** slope) + 1 for standing in range(1, amount + 1)]
    largest = most if full else min(most, max(-(-total // amount), total * loads[0] // sum(loads)))
    least = 1 if total - largest >= amount - 1 else 0
    holding, rest = [largest] + [least] * (amount - 1), total - largest - least * (amount - 1)
    while rest > 0:
        candidates = [i for i in range(1, amount) if holding[i] < largest] or [i for i in range(1, amount) if holding[i] < most]
        pool, budget = sum([loads[i] for i in candidates]), rest
        for i in candidates:
            more = min(most - holding[i], max(1, budget * loads[i] // pool), rest)
            holding[i] = holding[i] + more
            rest = rest - more
    return np.array(holding)


def scatter_about(stream_key, extent, spread, bound, split=(), kind=jnp.bfloat16):
    factor_of = steps_of(stream_key, extent, split, -0.22, 0.18) if split else 1.0
    values = jax.random.normal(stream_key, extent, jnp.float32) * spread * factor_of
    return jnp.minimum(jnp.maximum(values, -bound), bound).astype(kind)


def setup_inputs(seed: int = 0) -> dict:
    streams_of = jax.random.split(jax.random.key(seed), 8)
    x_rows = scatter_about(streams_of[0], (ROWS, D), 1.0, 6.0, ((0, 512),))
    expert_ids_keys = jax.random.split(jax.random.fold_in(streams_of[1], 1), ROWS // ROWS_DEV)
    expert_ids_turns = jax.random.permutation(jax.random.fold_in(streams_of[1], 3), ROWS // ROWS_DEV)
    expert_ids = jax.vmap(lambda own, number: assign_block(jax.random.fold_in(streams_of[1], 2), own, number, ROWS_DEV, EXPERTS, 1, CAP, 2))(expert_ids_keys, expert_ids_turns).reshape((ROWS, 1))
    gates = jnp.clip(jnp.exp(math.log(1.0) - 2.3025851 * jax.random.uniform(streams_of[2], (ROWS, 1), jnp.float32) ** steps_of(streams_of[2], (ROWS, 1), ((0, 512),), -0.2, 0.2)), 0.1, 1.0)
    cotangent = scatter_about(streams_of[3], (ROWS, D), 1.0, 6.0, ((0, 512),))
    w_gate = scatter_about(streams_of[4], (EXPERTS, D, HID), D ** -0.5, 0.1875, ((0, 128), (1, 4)))
    w_up = scatter_about(streams_of[5], (EXPERTS, D, HID), D ** -0.5, 0.1875, ((0, 128), (1, 4)))
    w_down = scatter_about(streams_of[6], (EXPERTS, HID, D), HID ** -0.5, 0.3125, ((0, 128), (2, 4)))
    return {"x_rows": x_rows, "expert_ids": expert_ids, "gates": gates, "cotangent": cotangent, "w_gate": w_gate, "w_up": w_up, "w_down": w_down}


def expert_rows(rows_in, rows_scaled, proj_gate, proj_up, proj_down):
    gate_act = jnp.dot(rows_in, proj_gate, preferred_element_type=jnp.float32)
    up_act = jnp.dot(rows_in, proj_up, preferred_element_type=jnp.float32)
    sigma = jax.nn.sigmoid(gate_act)
    hidden = (gate_act * sigma * up_act).astype(jnp.bfloat16)
    result = jnp.dot(hidden, proj_down, preferred_element_type=jnp.float32).astype(jnp.bfloat16)
    backed = jnp.dot(rows_scaled, proj_down.T, preferred_element_type=jnp.float32)
    d_gate_act = (backed * up_act * sigma * (1.0 + gate_act * (1.0 - sigma))).astype(jnp.bfloat16)
    d_up_act = (backed * gate_act * sigma).astype(jnp.bfloat16)
    d_input = (jnp.dot(d_gate_act, proj_gate.T, preferred_element_type=jnp.float32)
               + jnp.dot(d_up_act, proj_up.T, preferred_element_type=jnp.float32)).astype(jnp.bfloat16)
    grad_g = jnp.dot(rows_in.T, d_gate_act, preferred_element_type=jnp.float32)
    grad_u = jnp.dot(rows_in.T, d_up_act, preferred_element_type=jnp.float32)
    grad_d = jnp.dot(hidden.T, rows_scaled, preferred_element_type=jnp.float32)
    return result, d_input, (grad_g, grad_u, grad_d)


def group_pass(rows_in, rows_scaled, row_ids, w_gate, w_up, w_down):
    total = rows_in.shape[0]
    width = rows_in.shape[1]
    expert_count = w_gate.shape[0]
    onehot = (row_ids[:, None] == jnp.arange(expert_count, dtype=jnp.int32)[None, :]).astype(jnp.int32)
    counts = jnp.sum(onehot, 0)
    block_num = (counts + 127) // 128
    block_end = jnp.cumsum(block_num) * 128
    block_start = block_end - block_num * 128
    row_start = jnp.cumsum(counts) - counts
    order = jnp.argsort(row_ids, stable=True).astype(jnp.int32)
    sorted_ids = row_ids[order]
    target = (block_start[sorted_ids] + jnp.arange(total, dtype=jnp.int32) - row_start[sorted_ids]).astype(jnp.int32)
    padded = total + expert_count * 128
    nblocks = padded // 128
    source = jnp.full((padded,), total, jnp.int32).at[target].set(order)
    starts = jnp.arange(nblocks, dtype=jnp.int32) * 128
    block_expert = jnp.minimum(jnp.sum((block_end[None, :] <= starts[:, None]).astype(jnp.int32), 1), expert_count - 1).astype(jnp.int32)
    x_pad = jnp.concatenate([rows_in, jnp.zeros((1, width), rows_in.dtype)], 0)
    s_pad = jnp.concatenate([rows_scaled, jnp.zeros((1, width), rows_scaled.dtype)], 0)

    def advance(carry, item):
        block_rows, which = item
        result, d_input, grads = expert_rows(x_pad[block_rows], s_pad[block_rows], w_gate[which], w_up[which], w_down[which])
        carry = (carry[0].at[which].add(grads[0]), carry[1].at[which].add(grads[1]), carry[2].at[which].add(grads[2]))
        return carry, (result, d_input)

    hidden_units = w_gate.shape[2]
    init = (jnp.zeros((expert_count, width, hidden_units), jnp.float32),
            jnp.zeros((expert_count, width, hidden_units), jnp.float32),
            jnp.zeros((expert_count, hidden_units, width), jnp.float32))
    grads, (results, d_inputs) = lax.scan(advance, init, (source.reshape(nblocks, 128), block_expert))
    position = jnp.zeros((total,), jnp.int32).at[order].set(target)
    return results.reshape(padded, width)[position], d_inputs.reshape(padded, width)[position], grads


def reference(x_rows, expert_ids, gates, cotangent, w_gate, w_up, w_down):
    per_group = N_EXPERT * ROWS_DEV
    row_ids = expert_ids[:, 0].astype(jnp.int32)
    scaled = (gates * cotangent.astype(jnp.float32)).astype(jnp.bfloat16)
    results = []
    d_inputs = []
    summed = None
    for group in range(N_DP):
        lower = group * per_group
        upper = lower + per_group
        result, d_input, grads = group_pass(x_rows[lower:upper], scaled[lower:upper], row_ids[lower:upper], w_gate, w_up, w_down)
        results.append(result)
        d_inputs.append(d_input)
        rounded = lax.optimization_barrier(tuple(g.astype(jnp.bfloat16) for g in grads))
        rounded = tuple(g.astype(jnp.float32) for g in rounded)
        summed = rounded if summed is None else tuple(a + b for a, b in zip(summed, rounded))
    expert_out = jnp.concatenate(results, 0)
    input_grad = jnp.concatenate(d_inputs, 0)
    gated_out = (gates * expert_out.astype(jnp.float32)).astype(jnp.bfloat16)
    gate_grad = jnp.sum(cotangent.astype(jnp.float32) * expert_out.astype(jnp.float32), 1, keepdims=True)
    return (gated_out, input_grad, gate_grad, summed[0].astype(jnp.bfloat16),
            summed[1].astype(jnp.bfloat16), summed[2].astype(jnp.bfloat16))
```

```python
import jax
import jax.numpy as jnp
from jax import lax
from jax.experimental import pallas as pl
from jax.experimental.pallas import tpu as pltpu
from jax.sharding import PartitionSpec as P

BF = jnp.bfloat16
F32 = jnp.float32
VMEM = pl.BlockSpec(memory_space=pltpu.VMEM)
SMEM = pl.BlockSpec(memory_space=pltpu.SMEM)


def mm(a, b):
    return lax.dot_general(a, b, (((1,), (0,)), ((), ())), preferred_element_type=F32)


def mm_nt(a, b):
    return lax.dot_general(a, b, (((1,), (1,)), ((), ())), preferred_element_type=F32)


def mm_tn(a, b):
    return lax.dot_general(a, b, (((0,), (0,)), ((), ())), preferred_element_type=F32)


def source_of(o):
    return ((o >> 1) & 15) * 16 + (o & 1) * 8 + (o >> 5)


def sorting():
    rows = lax.broadcasted_iota(jnp.int32, (256, 256), 0)
    cols = lax.broadcasted_iota(jnp.int32, (256, 256), 1)
    return jnp.where(source_of(rows) == cols, 1.0, 0.0).astype(BF)


def unsorting():
    rows = lax.broadcasted_iota(jnp.int32, (256, 256), 0)
    cols = lax.broadcasted_iota(jnp.int32, (256, 256), 1)
    return jnp.where(source_of(cols) == rows, 1.0, 0.0).astype(BF)


def pack_weights_kernel(wg, wu, wd, out):
    out[0:256, :] = wg[0, :, 0:256]
    out[256:512, :] = wu[0, :, 0:256]
    out[512:768, 0:128] = wg[0, :, 256:384]
    out[512:768, 128:256] = wu[0, :, 256:384]
    out[768:1152, :] = wd[0]


def columns_of(row):
    return jnp.transpose(jnp.broadcast_to(row, (128, 128)))


def pack_rows_kernel(ids, gates, x, cot, send, place):
    row_ids = ids[...].astype(F32)
    across = jnp.broadcast_to(row_ids, (128, 128))
    down = jnp.transpose(across)
    earlier = lax.broadcasted_iota(jnp.int32, (128, 128), 0) < lax.broadcasted_iota(
        jnp.int32, (128, 128), 1
    )
    rank = jnp.sum(jnp.where((across == down) & earlier, 1.0, 0.0), axis=0, keepdims=True)
    slot = (row_ids * 2.0 + rank).astype(jnp.int32)
    onehot = jnp.where(
        lax.broadcasted_iota(jnp.int32, (256, 128), 0) == slot, 1.0, 0.0
    ).astype(BF)
    place[...] = onehot
    gate = columns_of(gates[...])
    back = unsorting()
    pieces = []
    for piece in range(4):
        pieces.append(mm(onehot, x[:, piece * 256 : piece * 256 + 256]).astype(BF))
    for piece in range(4):
        lower = cot[:, piece * 256 : piece * 256 + 128].astype(F32) * gate
        upper = cot[:, piece * 256 + 128 : piece * 256 + 256].astype(F32) * gate
        scaled = jnp.concatenate([lower, upper], 1).astype(BF)
        pieces.append(mm(onehot, scaled).astype(BF))
    for b in range(8):
        block = jnp.concatenate([p[b * 32 : b * 32 + 32, :] for p in pieces], 0)
        send[b * 256 : b * 256 + 256, :] = mm(back, block).astype(BF)


def expert_kernel(index, recv, w0, w1, w2, w3, send, g0, g1, g2, g3, rows, outs):
    me = index[0]
    sort = sorting()
    for b in range(8):
        block = mm(sort, recv[b * 256 : b * 256 + 256, :]).astype(BF)
        for piece in range(8):
            rows[piece, b * 32 : b * 32 + 32, :] = block[piece * 32 : piece * 32 + 32, :]
    shards = (w0, w1, w2, w3)
    gate_lo = up_lo = both_hi = backed = None
    for k in range(4):
        w = shards[k]
        q = (me + 4 - k) & 3
        xq = rows[q]
        sq = rows[4 + q]
        terms = (
            mm(xq, w[0:256, :]),
            mm(xq, w[256:512, :]),
            mm(xq, w[512:768, :]),
            mm_nt(sq, w[768:1152, :]),
        )
        if k == 0:
            gate_lo, up_lo, both_hi, backed = terms
        else:
            gate_lo, up_lo, both_hi, backed = (
                gate_lo + terms[0],
                up_lo + terms[1],
                both_hi + terms[2],
                backed + terms[3],
            )
    gate_act = jnp.concatenate([gate_lo, both_hi[:, 0:128]], 1)
    up_act = jnp.concatenate([up_lo, both_hi[:, 128:256]], 1)
    sigma = jax.nn.sigmoid(gate_act)
    hidden = (gate_act * sigma * up_act).astype(BF)
    d_gate = (backed * up_act * sigma * (1.0 + gate_act * (1.0 - sigma))).astype(BF)
    d_up = (backed * gate_act * sigma).astype(BF)
    dg_lo = d_gate[:, 0:256]
    du_lo = d_up[:, 0:256]
    d_hi = jnp.concatenate([d_gate[:, 256:384], d_up[:, 256:384]], 1)
    for k in range(4):
        w = shards[k]
        q = (me + 4 - k) & 3
        outs[q] = mm(hidden, w[768:1152, :]).astype(BF)
        outs[4 + q] = (
            mm_nt(dg_lo, w[0:256, :]) + mm_nt(du_lo, w[256:512, :]) + mm_nt(d_hi, w[512:768, :])
        ).astype(BF)
    back = unsorting()
    for b in range(8):
        block = jnp.concatenate([outs[p, b * 32 : b * 32 + 32, :] for p in range(8)], 0)
        send[b * 256 : b * 256 + 256, :] = mm(back, block).astype(BF)
    for k, g in enumerate((g0, g1, g2, g3)):
        q = (me + k) & 3
        xq = rows[q]
        sq = rows[4 + q]
        g[0:256, :] = mm_tn(xq, dg_lo).astype(BF)
        g[256:512, :] = mm_tn(xq, du_lo).astype(BF)
        g[512:768, :] = mm_tn(xq, d_hi).astype(BF)
        g[768:1152, :] = mm_tn(hidden, sq).astype(BF)


def unpack_kernel(recv, place, gates, cot, gated_out, input_grad, gate_grad, flat):
    sort = sorting()
    for b in range(8):
        block = mm(sort, recv[b * 256 : b * 256 + 256, :]).astype(BF)
        for piece in range(8):
            flat[b * 32 : b * 32 + 32, piece * 256 : piece * 256 + 256] = block[
                piece * 32 : piece * 32 + 32, :
            ]
    onehot = place[...]
    gate = columns_of(gates[...])
    total = jnp.zeros((128, 128), F32)
    row_out = mm_tn(onehot, flat[:, 0:1024])
    for part in range(8):
        cols = slice(part * 128, part * 128 + 128)
        piece = row_out[:, cols]
        gated_out[:, cols] = (gate * piece).astype(BF)
        total = total + cot[:, cols].astype(F32) * piece
    gate_grad[...] = jnp.sum(jnp.transpose(total), axis=0, keepdims=True)
    input_grad[...] = mm_tn(onehot, flat[:, 1024:2048]).astype(BF)


def sum_kernel(g0, r1, r2, r3, out_gate, out_up, out_down):
    def total(rows):
        return (
            g0[rows, :].astype(F32)
            + r1[rows, :].astype(F32)
            + r2[rows, :].astype(F32)
            + r3[rows, :].astype(F32)
        ).astype(BF)

    out_gate[0, :, 0:256] = total(slice(0, 256))
    out_up[0, :, 0:256] = total(slice(256, 512))
    both = total(slice(512, 768))
    out_gate[0, :, 256:384] = both[:, 0:128]
    out_up[0, :, 256:384] = both[:, 128:256]
    out_down[0] = total(slice(768, 1152))


def call(kernel, name, outs, specs, flops, moved, scratch=(), limit=24 << 20):
    return pl.pallas_call(
        kernel,
        name=name,
        out_shape=[jax.ShapeDtypeStruct(s, d) for s, d in outs],
        in_specs=specs,
        out_specs=[VMEM] * len(outs),
        scratch_shapes=list(scratch),
        cost_estimate=pl.CostEstimate(flops=flops, bytes_accessed=moved, transcendentals=0),
        compiler_params=pltpu.CompilerParams(vmem_limit_bytes=limit),
    )


def pack_weights(wg, wu, wd):
    return call(
        pack_weights_kernel, "pack_weights", [((1152, 256), BF)], [VMEM] * 3, 0, 1200000
    )(wg, wu, wd)[0]


def pack_rows(ids, gates, x, cot):
    return call(
        pack_rows_kernel,
        "pack_rows",
        [((2048, 256), BF), ((256, 128), BF)],
        [VMEM] * 4,
        400000000,
        1600000,
    )(ids, gates, x, cot)


def expert_rows(index, recv, shards):
    return call(
        expert_kernel,
        "expert_rows",
        [((2048, 256), BF)] + [((1152, 256), BF)] * 4,
        [SMEM] + [VMEM] * 5,
        2400000000,
        7000000,
        [pltpu.VMEM((8, 256, 256), BF), pltpu.VMEM((8, 256, 256), BF)],
        40 << 20,
    )(index, recv, *shards)


def unpack_rows(recv, place, gates, cot):
    return call(
        unpack_kernel,
        "unpack_rows",
        [((128, 1024), BF), ((128, 1024), BF), ((1, 128), F32)],
        [VMEM] * 4,
        400000000,
        2000000,
        [pltpu.VMEM((256, 2048), BF)],
    )(recv, place, gates, cot)


def sum_grads(parts):
    return call(
        sum_kernel,
        "sum_grads",
        [((1, 256, 384), BF), ((1, 256, 384), BF), ((1, 384, 256), BF)],
        [VMEM] * 4,
        0,
        3000000,
    )(*parts)


def per_device(x_rows, expert_ids, gates, cotangent, w_gate, w_up, w_down):
    groups = lax.axis_size("dp")

    def shift(value, k):
        return lax.ppermute(value, "dp", [(i, (i + k) % groups) for i in range(groups)])

    def exchange(rows):
        wire = rows.reshape(128, 16, 256)
        moved = lax.all_to_all(wire, "expert", split_axis=0, concat_axis=0, tiled=True)
        return moved.reshape(2048, 256)

    ids = expert_ids.reshape(1, 128)
    gate_row = gates.reshape(1, 128)
    own = pack_weights(w_gate, w_up, w_down)
    shards = [own] + [shift(own, k) for k in (1, 2, 3)]
    send, place = pack_rows(ids, gate_row, x_rows, cotangent)
    recv = exchange(send)
    index = lax.axis_index("dp").astype(jnp.int32).reshape(1)
    out = expert_rows(index, recv, shards)
    returned = exchange(out[0])
    parts = [out[1]] + [shift(out[1 + k], k) for k in (1, 2, 3)]
    gated_out, input_grad, gate_grad = unpack_rows(returned, place, gate_row, cotangent)
    grads = sum_grads(parts)
    return (gated_out, input_grad, gate_grad.reshape(128, 1), *grads)


def solution(mesh):
    in_specs = (
        P(("dp", "expert"), None),
        P(("dp", "expert"), None),
        P(("dp", "expert"), None),
        P(("dp", "expert"), None),
        P("expert", "dp", None),
        P("expert", "dp", None),
        P("expert", None, "dp"),
    )
    out_specs = (
        P(("dp", "expert"), None),
        P(("dp", "expert"), None),
        P(("dp", "expert"), None),
        P("expert", "dp", None),
        P("expert", "dp", None),
        P("expert", None, "dp"),
    )
    return jax.shard_map(
        per_device, mesh=mesh, in_specs=in_specs, out_specs=out_specs, check_vma=False
    )
```

```python
import jax
import jax.numpy as jnp
from jax import lax
from jax.experimental import pallas as pl
from jax.experimental.pallas import tpu as pltpu
from jax.sharding import PartitionSpec as P


BF = jnp.bfloat16
F32 = jnp.float32
VMEM = pl.BlockSpec(memory_space=pltpu.VMEM)
SMEM = pl.BlockSpec(memory_space=pltpu.SMEM)
HBM = pl.BlockSpec(memory_space=pltpu.HBM)


def mm(a, b):
    return lax.dot_general(a, b, (((1,), (0,)), ((), ())), preferred_element_type=F32)


def mm_nt(a, b):
    return lax.dot_general(a, b, (((1,), (1,)), ((), ())), preferred_element_type=F32)


def mm_tn(a, b):
    return lax.dot_general(a, b, (((0,), (0,)), ((), ())), preferred_element_type=F32)


def source_of(o):
    return ((o >> 1) & 15) * 16 + (o & 1) * 8 + (o >> 5)


def sorting():
    rows = lax.broadcasted_iota(jnp.int32, (256, 256), 0)
    cols = lax.broadcasted_iota(jnp.int32, (256, 256), 1)
    return jnp.where(source_of(rows) == cols, 1.0, 0.0).astype(BF)


def unsorting():
    rows = lax.broadcasted_iota(jnp.int32, (256, 256), 0)
    cols = lax.broadcasted_iota(jnp.int32, (256, 256), 1)
    return jnp.where(source_of(cols) == rows, 1.0, 0.0).astype(BF)


def columns_of(row):
    return jnp.transpose(jnp.broadcast_to(row, (128, 128)))


def weight_copies(wg, wu, wd, out, sems):
    return (
        pltpu.make_async_copy(wg.at[0, :, 0:256], out.at[0:256, :], sems.at[0]),
        pltpu.make_async_copy(wu.at[0, :, 0:256], out.at[256:512, :], sems.at[1]),
        pltpu.make_async_copy(wg.at[0, :, 256:384], out.at[512:768, 0:128], sems.at[2]),
        pltpu.make_async_copy(wu.at[0, :, 256:384], out.at[512:768, 128:256], sems.at[3]),
        pltpu.make_async_copy(wd.at[0], out.at[768:1152, :], sems.at[4]),
    )


def pack_kernel(
    ids, gates, x, cot, wg, wu, wd, own, send, place, ids_v, gates_v, x_v, cot_v, send_v, sems, out_sems
):
    small = (
        pltpu.make_async_copy(ids, ids_v, sems.at[5]),
        pltpu.make_async_copy(gates, gates_v, sems.at[6]),
    )
    large = (
        pltpu.make_async_copy(x, x_v, sems.at[7]),
        pltpu.make_async_copy(cot, cot_v, sems.at[8]),
    )
    weights = weight_copies(wg, wu, wd, own, sems)
    for copy in small + large + weights:
        copy.start()
    back = unsorting()
    for copy in small:
        copy.wait()
    row_ids = ids_v[...].astype(F32)
    across = jnp.broadcast_to(row_ids, (128, 128))
    down = jnp.transpose(across)
    earlier = lax.broadcasted_iota(jnp.int32, (128, 128), 0) < lax.broadcasted_iota(
        jnp.int32, (128, 128), 1
    )
    rank = jnp.sum(jnp.where((across == down) & earlier, 1.0, 0.0), axis=0, keepdims=True)
    slot = (row_ids * 2.0 + rank).astype(jnp.int32)
    onehot = jnp.where(
        lax.broadcasted_iota(jnp.int32, (256, 128), 0) == slot, 1.0, 0.0
    ).astype(BF)
    place[...] = onehot
    gate = columns_of(gates_v[...])
    pieces = []
    large[0].wait()
    for piece in range(4):
        pieces.append(mm(onehot, x_v[:, piece * 256 : piece * 256 + 256]).astype(BF))
    large[1].wait()
    for piece in range(4):
        lower = cot_v[:, piece * 256 : piece * 256 + 128].astype(F32) * gate
        upper = cot_v[:, piece * 256 + 128 : piece * 256 + 256].astype(F32) * gate
        scaled = jnp.concatenate([lower, upper], 1).astype(BF)
        pieces.append(mm(onehot, scaled).astype(BF))
    leaving = []
    for b in range(8):
        block = jnp.concatenate([p[b * 32 : b * 32 + 32, :] for p in pieces], 0)
        rows = pl.ds(b * 256, 256)
        send_v[rows, :] = mm(back, block).astype(BF)
        leaving.append(pltpu.make_async_copy(send_v.at[rows, :], send.at[rows, :], out_sems.at[b]))
        leaving[-1].start()
    for copy in weights:
        copy.wait()
    for copy in leaving:
        copy.wait()


def expert_kernel(
    index, recv, wg, wu, wd, w1, w2, w3, send, g0, g1, g2, g3,
    rows, outs, shards, send_v, grads_v, own_sems, in_sems, out_sems, grad_sems,
):
    me = index[0]
    arriving = [weight_copies(wg, wu, wd, shards.at[0], own_sems)]
    for k, w in enumerate((w1, w2, w3)):
        arriving.append((pltpu.make_async_copy(w, shards.at[k + 1], in_sems.at[k]),))
    for copies in arriving:
        for copy in copies:
            copy.start()
    sort = sorting()
    for b in range(8):
        block = mm(sort, recv[b * 256 : b * 256 + 256, :]).astype(BF)
        for piece in range(8):
            rows[piece, b * 32 : b * 32 + 32, :] = block[piece * 32 : piece * 32 + 32, :]
    gate_lo = up_lo = both_hi = backed = None
    for k in range(4):
        for copy in arriving[k]:
            copy.wait()
        q = (me + 4 - k) & 3
        xq = rows[q]
        sq = rows[4 + q]
        terms = (
            mm(xq, shards[k, 0:256, :]),
            mm(xq, shards[k, 256:512, :]),
            mm(xq, shards[k, 512:768, :]),
            mm_nt(sq, shards[k, 768:1152, :]),
        )
        if k == 0:
            gate_lo, up_lo, both_hi, backed = terms
        else:
            gate_lo, up_lo, both_hi, backed = (
                gate_lo + terms[0],
                up_lo + terms[1],
                both_hi + terms[2],
                backed + terms[3],
            )
    gate_act = jnp.concatenate([gate_lo, both_hi[:, 0:128]], 1)
    up_act = jnp.concatenate([up_lo, both_hi[:, 128:256]], 1)
    sigma = jax.nn.sigmoid(gate_act)
    hidden = (gate_act * sigma * up_act).astype(BF)
    d_gate = (backed * up_act * sigma * (1.0 + gate_act * (1.0 - sigma))).astype(BF)
    d_up = (backed * gate_act * sigma).astype(BF)
    dg_lo = d_gate[:, 0:256]
    du_lo = d_up[:, 0:256]
    d_hi = jnp.concatenate([d_gate[:, 256:384], d_up[:, 256:384]], 1)
    for k in range(4):
        q = (me + 4 - k) & 3
        outs[q] = mm(hidden, shards[k, 768:1152, :]).astype(BF)
        outs[4 + q] = (
            mm_nt(dg_lo, shards[k, 0:256, :])
            + mm_nt(du_lo, shards[k, 256:512, :])
            + mm_nt(d_hi, shards[k, 512:768, :])
        ).astype(BF)
    back = unsorting()
    leaving = []
    for b in range(8):
        block = jnp.concatenate([outs[p, b * 32 : b * 32 + 32, :] for p in range(8)], 0)
        part = pl.ds(b * 256, 256)
        send_v[part, :] = mm(back, block).astype(BF)
        leaving.append(pltpu.make_async_copy(send_v.at[part, :], send.at[part, :], out_sems.at[b]))
        leaving[-1].start()
    for k, g in ((2, g2), (1, g1), (3, g3), (0, g0)):
        q = (me + k) & 3
        xq = rows[q]
        sq = rows[4 + q]
        grads_v[k, 0:256, :] = mm_tn(xq, dg_lo).astype(BF)
        grads_v[k, 256:512, :] = mm_tn(xq, du_lo).astype(BF)
        grads_v[k, 512:768, :] = mm_tn(xq, d_hi).astype(BF)
        grads_v[k, 768:1152, :] = mm_tn(hidden, sq).astype(BF)
        leaving.append(pltpu.make_async_copy(grads_v.at[k], g, grad_sems.at[k]))
        leaving[-1].start()
    for copy in leaving:
        copy.wait()


def unpack_kernel(recv, place, gates, cot, gated_out, input_grad, gate_grad, flat):
    sort = sorting()
    for b in range(8):
        block = mm(sort, recv[b * 256 : b * 256 + 256, :]).astype(BF)
        for piece in range(8):
            flat[b * 32 : b * 32 + 32, piece * 256 : piece * 256 + 256] = block[
                piece * 32 : piece * 32 + 32, :
            ]
    onehot = place[...]
    gate = columns_of(gates[...])
    total = jnp.zeros((128, 128), F32)
    row_out = mm_tn(onehot, flat[:, 0:1024])
    for part in range(8):
        cols = slice(part * 128, part * 128 + 128)
        piece = row_out[:, cols]
        gated_out[:, cols] = (gate * piece).astype(BF)
        total = total + cot[:, cols].astype(F32) * piece
    gate_grad[...] = jnp.sum(jnp.transpose(total), axis=0, keepdims=True)
    input_grad[...] = mm_tn(onehot, flat[:, 1024:2048]).astype(BF)


def sum_kernel(g0, r1, r2, r3, out_gate, out_up, out_down):
    def total(rows):
        return (
            g0[rows, :].astype(F32)
            + r1[rows, :].astype(F32)
            + r2[rows, :].astype(F32)
            + r3[rows, :].astype(F32)
        ).astype(BF)

    out_gate[0, :, 0:256] = total(slice(0, 256))
    out_up[0, :, 0:256] = total(slice(256, 512))
    both = total(slice(512, 768))
    out_gate[0, :, 256:384] = both[:, 0:128]
    out_up[0, :, 256:384] = both[:, 128:256]
    out_down[0] = total(slice(768, 1152))


def call(kernel, outs, specs, out_specs, flops, moved, scratch=(), limit=12 << 20):
    return pl.pallas_call(
        kernel,
        out_shape=[jax.ShapeDtypeStruct(s, d) for s, d in outs],
        in_specs=specs,
        out_specs=out_specs,
        scratch_shapes=list(scratch),
        cost_estimate=pl.CostEstimate(flops=flops, bytes_accessed=moved, transcendentals=0),
        compiler_params=pltpu.CompilerParams(vmem_limit_bytes=limit),
    )


def hbm(x):
    return pltpu.with_memory_space_constraint(x, pltpu.HBM)


def pack(ids, gates, x, cot, wg, wu, wd):
    return call(
        pack_kernel,
        [((1152, 256), BF), ((2048, 256), BF), ((256, 128), BF)],
        [HBM] * 7,
        [VMEM, HBM, VMEM],
        400000000,
        2600000,
        [
            pltpu.VMEM((1, 128), jnp.int32),
            pltpu.VMEM((1, 128), F32),
            pltpu.VMEM((128, 1024), BF),
            pltpu.VMEM((128, 1024), BF),
            pltpu.VMEM((2048, 256), BF),
            pltpu.SemaphoreType.DMA((9,)),
            pltpu.SemaphoreType.DMA((8,)),
        ],
    )(*map(hbm, (ids, gates, x, cot, wg, wu, wd)))


def expert_rows(index, recv, wg, wu, wd, shards):
    return call(
        expert_kernel,
        [((2048, 256), BF)] + [((1152, 256), BF)] * 4,
        [SMEM, VMEM] + [HBM] * 6,
        [HBM] * 5,
        2400000000,
        7000000,
        [
            pltpu.VMEM((8, 256, 256), BF),
            pltpu.VMEM((8, 256, 256), BF),
            pltpu.VMEM((4, 1152, 256), BF),
            pltpu.VMEM((2048, 256), BF),
            pltpu.VMEM((4, 1152, 256), BF),
            pltpu.SemaphoreType.DMA((5,)),
            pltpu.SemaphoreType.DMA((3,)),
            pltpu.SemaphoreType.DMA((8,)),
            pltpu.SemaphoreType.DMA((4,)),
        ],
        24 << 20,
    )(index, recv, *map(hbm, (wg, wu, wd, *shards)))


def unpack_rows(recv, place, gates, cot):
    return call(
        unpack_kernel,
        [((128, 1024), BF), ((128, 1024), BF), ((1, 128), F32)],
        [VMEM] * 4,
        [VMEM] * 3,
        400000000,
        2000000,
        [pltpu.VMEM((256, 2048), BF)],
    )(recv, place, gates, cot)


def sum_grads(parts):
    return call(
        sum_kernel,
        [((1, 256, 384), BF), ((1, 256, 384), BF), ((1, 384, 256), BF)],
        [VMEM] * 4,
        [VMEM] * 3,
        0,
        3000000,
    )(*parts)


def per_device(x_rows, expert_ids, gates, cotangent, w_gate, w_up, w_down):
    groups = lax.axis_size("dp")

    def shift(value, k):
        return lax.ppermute(value, "dp", [(i, (i + k) % groups) for i in range(groups)])

    def exchange(rows):
        wire = rows.reshape(128, 16, 256)
        moved = lax.all_to_all(wire, "expert", split_axis=0, concat_axis=0, tiled=True)
        return moved.reshape(2048, 256)

    ids = expert_ids.reshape(1, 128)
    gate_row = gates.reshape(1, 128)
    own, send, place = pack(ids, gate_row, x_rows, cotangent, w_gate, w_up, w_down)
    shards = []
    for k in (1, 2, 3):
        shards.append(shift(own, k))
    recv = exchange(send)
    index = lax.axis_index("dp").astype(jnp.int32).reshape(1)
    out = expert_rows(index, recv, w_gate, w_up, w_down, shards)
    returned = exchange(out[0])
    parts = [out[1]]
    for k in (1, 2, 3):
        parts.append(shift(out[1 + k], k))
    gated_out, input_grad, gate_grad = unpack_rows(returned, place, gate_row, cotangent)
    grads = sum_grads(parts)
    return (gated_out, input_grad, gate_grad.reshape(128, 1), *grads)


def solution(mesh):
    in_specs = (
        P(("dp", "expert"), None),
        P(("dp", "expert"), None),
        P(("dp", "expert"), None),
        P(("dp", "expert"), None),
        P("expert", "dp", None),
        P("expert", "dp", None),
        P("expert", None, "dp"),
    )
    out_specs = (
        P(("dp", "expert"), None),
        P(("dp", "expert"), None),
        P(("dp", "expert"), None),
        P("expert", "dp", None),
        P("expert", "dp", None),
        P("expert", None, "dp"),
    )
    return jax.shard_map(
        per_device, mesh=mesh, in_specs=in_specs, out_specs=out_specs, check_vma=False
    )
```

```python
import jax
import jax.numpy as jnp
from jax import lax
from jax.experimental import pallas as pl
from jax.experimental.pallas import tpu as pltpu
from jax.sharding import PartitionSpec as P


BF = jnp.bfloat16
F32 = jnp.float32
VMEM = pl.BlockSpec(memory_space=pltpu.VMEM)
SMEM = pl.BlockSpec(memory_space=pltpu.SMEM)
HBM = pl.BlockSpec(memory_space=pltpu.HBM)


def mm(a, b):
    return lax.dot_general(a, b, (((1,), (0,)), ((), ())), preferred_element_type=F32)


def mm_nt(a, b):
    return lax.dot_general(a, b, (((1,), (1,)), ((), ())), preferred_element_type=F32)


def mm_tn(a, b):
    return lax.dot_general(a, b, (((0,), (0,)), ((), ())), preferred_element_type=F32)


def source_of(o):
    return ((o >> 1) & 15) * 16 + (o & 1) * 8 + (o >> 5)


def sorting():
    rows = lax.broadcasted_iota(jnp.int32, (256, 256), 0)
    cols = lax.broadcasted_iota(jnp.int32, (256, 256), 1)
    return jnp.where(source_of(rows) == cols, 1.0, 0.0).astype(BF)


def unsorting():
    rows = lax.broadcasted_iota(jnp.int32, (256, 256), 0)
    cols = lax.broadcasted_iota(jnp.int32, (256, 256), 1)
    return jnp.where(source_of(cols) == rows, 1.0, 0.0).astype(BF)


def columns_of(row):
    return jnp.transpose(jnp.broadcast_to(row, (128, 128)))


def weight_copies(wg, wu, wd, out, sems):
    return (
        pltpu.make_async_copy(wg.at[0, :, 0:256], out.at[0:256, :], sems.at[0]),
        pltpu.make_async_copy(wu.at[0, :, 0:256], out.at[256:512, :], sems.at[1]),
        pltpu.make_async_copy(wg.at[0, :, 256:384], out.at[512:768, 0:128], sems.at[2]),
        pltpu.make_async_copy(wu.at[0, :, 256:384], out.at[512:768, 128:256], sems.at[3]),
        pltpu.make_async_copy(wd.at[0], out.at[768:1152, :], sems.at[4]),
    )


def pack_kernel(
    ids, gates, x, cot, wg, wu, wd, own, send, place, ids_v, gates_v, x_v, cot_v, send_v, sems, out_sems
):
    small = (
        pltpu.make_async_copy(ids, ids_v, sems.at[5]),
        pltpu.make_async_copy(gates, gates_v, sems.at[6]),
    )
    large = (
        pltpu.make_async_copy(x, x_v, sems.at[7]),
        pltpu.make_async_copy(cot, cot_v, sems.at[8]),
    )
    weights = weight_copies(wg, wu, wd, own, sems)
    for copy in small + large + weights:
        copy.start()
    back = unsorting()
    for copy in small:
        copy.wait()
    row_ids = ids_v[...].astype(F32)
    across = jnp.broadcast_to(row_ids, (128, 128))
    down = jnp.transpose(across)
    earlier = lax.broadcasted_iota(jnp.int32, (128, 128), 0) < lax.broadcasted_iota(
        jnp.int32, (128, 128), 1
    )
    rank = jnp.sum(jnp.where((across == down) & earlier, 1.0, 0.0), axis=0, keepdims=True)
    slot = (row_ids * 2.0 + rank).astype(jnp.int32)
    onehot = jnp.where(
        lax.broadcasted_iota(jnp.int32, (256, 128), 0) == slot, 1.0, 0.0
    ).astype(BF)
    place[...] = onehot
    gate = columns_of(gates_v[...])
    pieces = []
    large[0].wait()
    for piece in range(4):
        pieces.append(mm(onehot, x_v[:, piece * 256 : piece * 256 + 256]).astype(BF))
    large[1].wait()
    for piece in range(4):
        lower = cot_v[:, piece * 256 : piece * 256 + 128].astype(F32) * gate
        upper = cot_v[:, piece * 256 + 128 : piece * 256 + 256].astype(F32) * gate
        scaled = jnp.concatenate([lower, upper], 1).astype(BF)
        pieces.append(mm(onehot, scaled).astype(BF))
    leaving = []
    for b in range(8):
        block = jnp.concatenate([p[b * 32 : b * 32 + 32, :] for p in pieces], 0)
        rows = pl.ds(b * 256, 256)
        send_v[rows, :] = mm(back, block).astype(BF)
        leaving.append(pltpu.make_async_copy(send_v.at[rows, :], send.at[rows, :], out_sems.at[b]))
        leaving[-1].start()
    for copy in weights:
        copy.wait()
    for copy in leaving:
        copy.wait()


def expert_kernel(
    index, recv, wg, wu, wd, w1, w2, w3, send, g2, rows_out, slopes_out, hidden_out,
    outs, w0, send_v, g2_v, rows, slopes, hidden_v, own_sems, out_sems,
):
    me = index[0]
    arriving = weight_copies(wg, wu, wd, w0, own_sems)
    for copy in arriving:
        copy.start()
    sort = sorting()
    for b in range(8):
        block = mm(sort, recv[b * 256 : b * 256 + 256, :]).astype(BF)
        for piece in range(8):
            rows[piece, b * 32 : b * 32 + 32, :] = block[piece * 32 : piece * 32 + 32, :]
    gate_lo = up_lo = both_hi = backed = None
    leaving = [pltpu.make_async_copy(rows, rows_out, out_sems.at[8])]
    leaving[0].start()
    shards = (w0, w1, w2, w3)
    for k in (1, 2, 3, 0):
        if k == 0:
            for copy in arriving:
                copy.wait()
        w = shards[k]
        q = (me + 4 - k) & 3
        xq = rows[q]
        sq = rows[4 + q]
        terms = (
            mm(xq, w[0:256, :]),
            mm(xq, w[256:512, :]),
            mm(xq, w[512:768, :]),
            mm_nt(sq, w[768:1152, :]),
        )
        if k == 1:
            gate_lo, up_lo, both_hi, backed = terms
        else:
            gate_lo, up_lo, both_hi, backed = (
                gate_lo + terms[0],
                up_lo + terms[1],
                both_hi + terms[2],
                backed + terms[3],
            )
    gate_act = jnp.concatenate([gate_lo, both_hi[:, 0:128]], 1)
    up_act = jnp.concatenate([up_lo, both_hi[:, 128:256]], 1)
    sigma = jax.nn.sigmoid(gate_act)
    hidden = (gate_act * sigma * up_act).astype(BF)
    d_gate = (backed * up_act * sigma * (1.0 + gate_act * (1.0 - sigma))).astype(BF)
    d_up = (backed * gate_act * sigma).astype(BF)
    dg_lo = d_gate[:, 0:256]
    du_lo = d_up[:, 0:256]
    d_hi = jnp.concatenate([d_gate[:, 256:384], d_up[:, 256:384]], 1)
    hidden_v[...] = hidden
    slopes[0] = dg_lo
    slopes[1] = du_lo
    slopes[2] = d_hi
    grads_of((me + 2) & 3, g2_v, rows, slopes, hidden_v)
    for n, (source, target) in enumerate(
        ((hidden_v, hidden_out), (slopes, slopes_out), (g2_v, g2))
    ):
        leaving.append(pltpu.make_async_copy(source, target, out_sems.at[9 + n]))
        leaving[-1].start()
    for k in range(4):
        q = (me + 4 - k) & 3
        w = shards[k]
        outs[q] = mm(hidden, w[768:1152, :]).astype(BF)
        outs[4 + q] = (
            mm_nt(dg_lo, w[0:256, :]) + mm_nt(du_lo, w[256:512, :]) + mm_nt(d_hi, w[512:768, :])
        ).astype(BF)
    back = unsorting()
    for b in range(8):
        block = jnp.concatenate([outs[p, b * 32 : b * 32 + 32, :] for p in range(8)], 0)
        part = pl.ds(b * 256, 256)
        send_v[part, :] = mm(back, block).astype(BF)
        leaving.append(pltpu.make_async_copy(send_v.at[part, :], send.at[part, :], out_sems.at[b]))
        leaving[-1].start()
    for copy in leaving:
        copy.wait()


def grads_of(q, out, rows, slopes, hidden):
    for part in range(3):
        out[part * 256 : part * 256 + 256, :] = mm_tn(rows[q], slopes[part]).astype(BF)
    out[768:1152, :] = mm_tn(hidden[...], rows[4 + q]).astype(BF)


def grads_kernel(index, rows, slopes, hidden, g1, g3, g0):
    me = index[0]
    for k, g in ((1, g1), (3, g3), (0, g0)):
        grads_of((me + k) & 3, g, rows, slopes, hidden)


def unpack_kernel(
    recv, place, gates_hbm, cot_hbm, gated_out, input_grad, gate_grad,
    flat, gates, cot, gated_v, input_v, in_sems, out_sems,
):
    arriving = (
        pltpu.make_async_copy(gates_hbm, gates, in_sems.at[0]),
        pltpu.make_async_copy(cot_hbm, cot, in_sems.at[1]),
    )
    for copy in arriving:
        copy.start()
    sort = sorting()
    for b in range(8):
        block = mm(sort, recv[b * 256 : b * 256 + 256, :]).astype(BF)
        for piece in range(8):
            flat[b * 32 : b * 32 + 32, piece * 256 : piece * 256 + 256] = block[
                piece * 32 : piece * 32 + 32, :
            ]
    onehot = place[...]
    input_v[...] = mm_tn(onehot, flat[:, 1024:2048]).astype(BF)
    leaving = [pltpu.make_async_copy(input_v, input_grad, out_sems.at[0])]
    leaving[0].start()
    row_out = mm_tn(onehot, flat[:, 0:1024])
    for copy in arriving:
        copy.wait()
    gate = columns_of(gates[...])
    total = jnp.zeros((128, 128), F32)
    for part in range(8):
        cols = slice(part * 128, part * 128 + 128)
        piece = row_out[:, cols]
        gated_v[:, cols] = (gate * piece).astype(BF)
        total = total + cot[:, cols].astype(F32) * piece
    leaving.append(pltpu.make_async_copy(gated_v, gated_out, out_sems.at[1]))
    leaving[1].start()
    gate_grad[...] = jnp.sum(jnp.transpose(total), axis=0, keepdims=True)
    for copy in leaving:
        copy.wait()


def sum_kernel(g0, r1, r2, r3, out_gate, out_up, out_down):
    def total(rows):
        return (
            g0[rows, :].astype(F32)
            + r1[rows, :].astype(F32)
            + r2[rows, :].astype(F32)
            + r3[rows, :].astype(F32)
        ).astype(BF)

    out_gate[0, :, 0:256] = total(slice(0, 256))
    out_up[0, :, 0:256] = total(slice(256, 512))
    both = total(slice(512, 768))
    out_gate[0, :, 256:384] = both[:, 0:128]
    out_up[0, :, 256:384] = both[:, 128:256]
    out_down[0] = total(slice(768, 1152))


def call(kernel, outs, specs, out_specs, flops, moved, scratch=(), limit=12 << 20):
    return pl.pallas_call(
        kernel,
        out_shape=[
            pltpu.HBM(o[0], o[1]) if len(o) == 3 else jax.ShapeDtypeStruct(*o) for o in outs
        ],
        in_specs=specs,
        out_specs=out_specs,
        scratch_shapes=list(scratch),
        cost_estimate=pl.CostEstimate(flops=flops, bytes_accessed=moved, transcendentals=0),
        compiler_params=pltpu.CompilerParams(vmem_limit_bytes=limit),
    )


def hbm(x):
    return pltpu.with_memory_space_constraint(x, pltpu.HBM)


def pack(ids, gates, x, cot, wg, wu, wd):
    return call(
        pack_kernel,
        [((1152, 256), BF), ((2048, 256), BF), ((256, 128), BF)],
        [HBM] * 7,
        [VMEM, HBM, VMEM],
        400000000,
        2600000,
        [
            pltpu.VMEM((1, 128), jnp.int32),
            pltpu.VMEM((1, 128), F32),
            pltpu.VMEM((128, 1024), BF),
            pltpu.VMEM((128, 1024), BF),
            pltpu.VMEM((2048, 256), BF),
            pltpu.SemaphoreType.DMA((9,)),
            pltpu.SemaphoreType.DMA((8,)),
        ],
    )(*map(hbm, (ids, gates, x, cot, wg, wu, wd)))


def expert_rows(index, recv, wg, wu, wd, shards):
    return call(
        expert_kernel,
        [
            ((2048, 256), BF),
            ((1152, 256), BF, True),
            ((8, 256, 256), BF, True),
            ((3, 256, 256), BF, True),
            ((256, 384), BF, True),
        ],
        [SMEM, VMEM] + [HBM] * 3 + [VMEM] * 3,
        [HBM] * 5,
        2000000000,
        6000000,
        [
            pltpu.VMEM((8, 256, 256), BF),
            pltpu.VMEM((1152, 256), BF),
            pltpu.VMEM((2048, 256), BF),
            pltpu.VMEM((1152, 256), BF),
            pltpu.VMEM((8, 256, 256), BF),
            pltpu.VMEM((3, 256, 256), BF),
            pltpu.VMEM((256, 384), BF),
            pltpu.SemaphoreType.DMA((5,)),
            pltpu.SemaphoreType.DMA((12,)),
        ],
        24 << 20,
    )(index, recv, *map(hbm, (wg, wu, wd)), *shards)


def other_grads(index, rows, slopes, hidden):
    return call(
        grads_kernel, [((1152, 256), BF)] * 3, [SMEM] + [VMEM] * 3, [VMEM] * 3, 450000000, 3000000
    )(index, rows, slopes, hidden)


def unpack_rows(recv, place, gates, cot):
    return call(
        unpack_kernel,
        [((128, 1024), BF), ((128, 1024), BF), ((1, 128), F32)],
        [VMEM, VMEM, HBM, HBM],
        [HBM, HBM, VMEM],
        400000000,
        2000000,
        [
            pltpu.VMEM((256, 2048), BF),
            pltpu.VMEM((1, 128), F32),
            pltpu.VMEM((128, 1024), BF),
            pltpu.VMEM((128, 1024), BF),
            pltpu.VMEM((128, 1024), BF),
            pltpu.SemaphoreType.DMA((2,)),
            pltpu.SemaphoreType.DMA((2,)),
        ],
    )(recv, place, hbm(gates), hbm(cot))


def sum_grads(parts):
    return call(
        sum_kernel,
        [((1, 256, 384), BF), ((1, 256, 384), BF), ((1, 384, 256), BF)],
        [VMEM] * 4,
        [VMEM] * 3,
        0,
        3000000,
    )(*parts)


def per_device(x_rows, expert_ids, gates, cotangent, w_gate, w_up, w_down):
    groups = lax.axis_size("dp")

    def shift(value, k):
        return lax.ppermute(value, "dp", [(i, (i + k) % groups) for i in range(groups)])

    def exchange(rows):
        wire = rows.reshape(128, 16, 256)
        moved = lax.all_to_all(wire, "expert", split_axis=0, concat_axis=0, tiled=True)
        return moved.reshape(2048, 256)

    ids = expert_ids.reshape(1, 128)
    gate_row = gates.reshape(1, 128)
    own, send, place = pack(ids, gate_row, x_rows, cotangent, w_gate, w_up, w_down)
    shards = []
    for k in (1, 2, 3):
        shards.append(shift(own, k))
    recv = exchange(send)
    index = lax.axis_index("dp").astype(jnp.int32).reshape(1)
    out, g2, rows, slopes, hidden = expert_rows(index, recv, w_gate, w_up, w_down, shards)
    returned = exchange(out)
    r2 = shift(g2, 2)
    g1, g3, g0 = other_grads(index, rows, slopes, hidden)
    r1 = shift(g1, 1)
    r3 = shift(g3, 3)
    parts = (g0, r1, r2, r3)
    gated_out, input_grad, gate_grad = unpack_rows(returned, place, gate_row, cotangent)
    grads = sum_grads(parts)
    return (gated_out, input_grad, gate_grad.reshape(128, 1), *grads)


def solution(mesh):
    in_specs = (
        P(("dp", "expert"), None),
        P(("dp", "expert"), None),
        P(("dp", "expert"), None),
        P(("dp", "expert"), None),
        P("expert", "dp", None),
        P("expert", "dp", None),
        P("expert", None, "dp"),
    )
    out_specs = (
        P(("dp", "expert"), None),
        P(("dp", "expert"), None),
        P(("dp", "expert"), None),
        P("expert", "dp", None),
        P("expert", "dp", None),
        P("expert", None, "dp"),
    )
    return jax.shard_map(
        per_device, mesh=mesh, in_specs=in_specs, out_specs=out_specs, check_vma=False
    )
```

```python
import jax
import jax.numpy as jnp
from jax import lax
from jax.experimental import pallas as pl
from jax.experimental.pallas import tpu as pltpu
from jax.sharding import PartitionSpec as P


BF = jnp.bfloat16
F32 = jnp.float32
VMEM = pl.BlockSpec(memory_space=pltpu.VMEM)
SMEM = pl.BlockSpec(memory_space=pltpu.SMEM)
HBM = pl.BlockSpec(memory_space=pltpu.HBM)


def mm(a, b):
    return lax.dot_general(a, b, (((1,), (0,)), ((), ())), preferred_element_type=F32)


def mm_nt(a, b):
    return lax.dot_general(a, b, (((1,), (1,)), ((), ())), preferred_element_type=F32)


def mm_tn(a, b):
    return lax.dot_general(a, b, (((0,), (0,)), ((), ())), preferred_element_type=F32)


def source_of(o):
    return ((o >> 1) & 15) * 16 + (o & 1) * 8 + (o >> 5)


def sorting():
    rows = lax.broadcasted_iota(jnp.int32, (256, 256), 0)
    cols = lax.broadcasted_iota(jnp.int32, (256, 256), 1)
    return jnp.where(source_of(rows) == cols, 1.0, 0.0).astype(BF)


def unsorting():
    rows = lax.broadcasted_iota(jnp.int32, (256, 256), 0)
    cols = lax.broadcasted_iota(jnp.int32, (256, 256), 1)
    return jnp.where(source_of(cols) == rows, 1.0, 0.0).astype(BF)


def columns_of(row):
    return jnp.transpose(jnp.broadcast_to(row, (128, 128)))


def weight_copies(wg, wu, wd, out, sems):
    return (
        pltpu.make_async_copy(wg.at[0, :, 0:256], out.at[0:256, :], sems.at[0]),
        pltpu.make_async_copy(wu.at[0, :, 0:256], out.at[256:512, :], sems.at[1]),
        pltpu.make_async_copy(wg.at[0, :, 256:384], out.at[512:768, 0:128], sems.at[2]),
        pltpu.make_async_copy(wu.at[0, :, 256:384], out.at[512:768, 128:256], sems.at[3]),
        pltpu.make_async_copy(wd.at[0], out.at[768:1152, :], sems.at[4]),
    )


def pack_kernel(
    ids, gates, x, cot, wg, wu, wd, own, send, place, gates_v, ids_v, x_v, cot_v, send_v, sems, out_sems
):
    small = (
        pltpu.make_async_copy(ids, ids_v, sems.at[5]),
        pltpu.make_async_copy(gates, gates_v, sems.at[6]),
    )
    large = (
        pltpu.make_async_copy(x, x_v, sems.at[7]),
        pltpu.make_async_copy(cot, cot_v, sems.at[8]),
    )
    weights = weight_copies(wg, wu, wd, own, sems)
    for copy in small + large + weights:
        copy.start()
    back = unsorting()
    for copy in small:
        copy.wait()
    row_ids = ids_v[...].astype(F32)
    across = jnp.broadcast_to(row_ids, (128, 128))
    down = jnp.transpose(across)
    earlier = lax.broadcasted_iota(jnp.int32, (128, 128), 0) < lax.broadcasted_iota(
        jnp.int32, (128, 128), 1
    )
    rank = jnp.sum(jnp.where((across == down) & earlier, 1.0, 0.0), axis=0, keepdims=True)
    slot = (row_ids * 2.0 + rank).astype(jnp.int32)
    onehot = jnp.where(
        lax.broadcasted_iota(jnp.int32, (256, 128), 0) == slot, 1.0, 0.0
    ).astype(BF)
    place[...] = onehot
    gate = columns_of(gates_v[...])
    pieces = []
    large[0].wait()
    for piece in range(4):
        pieces.append(mm(onehot, x_v[:, piece * 256 : piece * 256 + 256]).astype(BF))
    large[1].wait()
    for piece in range(4):
        lower = cot_v[:, piece * 256 : piece * 256 + 128].astype(F32) * gate
        upper = cot_v[:, piece * 256 + 128 : piece * 256 + 256].astype(F32) * gate
        scaled = jnp.concatenate([lower, upper], 1).astype(BF)
        pieces.append(mm(onehot, scaled).astype(BF))
    leaving = []
    for b in range(8):
        block = jnp.concatenate([p[b * 32 : b * 32 + 32, :] for p in pieces], 0)
        rows = pl.ds(b * 256, 256)
        send_v[rows, :] = mm(back, block).astype(BF)
        leaving.append(pltpu.make_async_copy(send_v.at[rows, :], send.at[rows, :], out_sems.at[b]))
        leaving[-1].start()
    for copy in weights:
        copy.wait()
    for copy in leaving:
        copy.wait()


def expert_kernel(
    index, recv, w0, w1, w2, w3, send, g2, rows_out, slopes_out, hidden_out,
    outs, send_v, g2_v, rows, slopes, hidden_v, out_sems,
):
    me = index[0]
    sort = sorting()
    for b in range(8):
        block = mm(sort, recv[b * 256 : b * 256 + 256, :]).astype(BF)
        for piece in range(8):
            rows[piece, b * 32 : b * 32 + 32, :] = block[piece * 32 : piece * 32 + 32, :]
    gate_lo = up_lo = both_hi = backed = None
    leaving = [pltpu.make_async_copy(rows, rows_out, out_sems.at[8])]
    leaving[0].start()
    shards = (w0, w1, w2, w3)
    for k in range(4):
        w = shards[k]
        q = (me + 4 - k) & 3
        xq = rows[q]
        sq = rows[4 + q]
        terms = (
            mm(xq, w[0:256, :]),
            mm(xq, w[256:512, :]),
            mm(xq, w[512:768, :]),
            mm_nt(sq, w[768:1152, :]),
        )
        if k == 0:
            gate_lo, up_lo, both_hi, backed = terms
        else:
            gate_lo, up_lo, both_hi, backed = (
                gate_lo + terms[0],
                up_lo + terms[1],
                both_hi + terms[2],
                backed + terms[3],
            )
    gate_act = jnp.concatenate([gate_lo, both_hi[:, 0:128]], 1)
    up_act = jnp.concatenate([up_lo, both_hi[:, 128:256]], 1)
    sigma = jax.nn.sigmoid(gate_act)
    hidden = (gate_act * sigma * up_act).astype(BF)
    d_gate = (backed * up_act * sigma * (1.0 + gate_act * (1.0 - sigma))).astype(BF)
    d_up = (backed * gate_act * sigma).astype(BF)
    dg_lo = d_gate[:, 0:256]
    du_lo = d_up[:, 0:256]
    d_hi = jnp.concatenate([d_gate[:, 256:384], d_up[:, 256:384]], 1)
    hidden_v[...] = hidden
    slopes[0] = dg_lo
    slopes[1] = du_lo
    slopes[2] = d_hi
    grads_of((me + 2) & 3, g2_v, rows, slopes, hidden_v)
    for n, (source, target) in enumerate(
        ((hidden_v, hidden_out), (slopes, slopes_out), (g2_v, g2))
    ):
        leaving.append(pltpu.make_async_copy(source, target, out_sems.at[9 + n]))
        leaving[-1].start()
    for k in range(4):
        q = (me + 4 - k) & 3
        w = shards[k]
        outs[q] = mm(hidden, w[768:1152, :]).astype(BF)
        outs[4 + q] = (
            mm_nt(dg_lo, w[0:256, :]) + mm_nt(du_lo, w[256:512, :]) + mm_nt(d_hi, w[512:768, :])
        ).astype(BF)
    back = unsorting()
    for b in range(8):
        block = jnp.concatenate([outs[p, b * 32 : b * 32 + 32, :] for p in range(8)], 0)
        part = pl.ds(b * 256, 256)
        send_v[part, :] = mm(back, block).astype(BF)
        leaving.append(pltpu.make_async_copy(send_v.at[part, :], send.at[part, :], out_sems.at[b]))
        leaving[-1].start()
    for copy in leaving:
        copy.wait()


def grads_of(q, out, rows, slopes, hidden):
    for part in range(3):
        out[part * 256 : part * 256 + 256, :] = mm_tn(rows[q], slopes[part]).astype(BF)
    out[768:1152, :] = mm_tn(hidden[...], rows[4 + q]).astype(BF)


def grads_kernel(index, rows, slopes, hidden, g1, g3, g0):
    me = index[0]
    for k, g in ((1, g1), (3, g3), (0, g0)):
        grads_of((me + k) & 3, g, rows, slopes, hidden)


def unpack_kernel(recv, place, gates, cot, gated_out, input_grad, gate_grad, flat):
    sort = sorting()
    for b in range(8):
        block = mm(sort, recv[b * 256 : b * 256 + 256, :]).astype(BF)
        for piece in range(8):
            flat[b * 32 : b * 32 + 32, piece * 256 : piece * 256 + 256] = block[
                piece * 32 : piece * 32 + 32, :
            ]
    onehot = place[...]
    gate = columns_of(gates[...])
    total = jnp.zeros((128, 128), F32)
    row_out = mm_tn(onehot, flat[:, 0:1024])
    for part in range(8):
        cols = slice(part * 128, part * 128 + 128)
        piece = row_out[:, cols]
        gated_out[:, cols] = (gate * piece).astype(BF)
        total = total + cot[:, cols].astype(F32) * piece
    gate_grad[...] = jnp.sum(jnp.transpose(total), axis=0, keepdims=True)
    input_grad[...] = mm_tn(onehot, flat[:, 1024:2048]).astype(BF)


def sum_kernel(g0, r1, r2, r3, out_gate, out_up, out_down):
    def total(rows):
        return (
            g0[rows, :].astype(F32)
            + r1[rows, :].astype(F32)
            + r2[rows, :].astype(F32)
            + r3[rows, :].astype(F32)
        ).astype(BF)

    out_gate[0, :, 0:256] = total(slice(0, 256))
    out_up[0, :, 0:256] = total(slice(256, 512))
    both = total(slice(512, 768))
    out_gate[0, :, 256:384] = both[:, 0:128]
    out_up[0, :, 256:384] = both[:, 128:256]
    out_down[0] = total(slice(768, 1152))


def call(kernel, outs, specs, out_specs, flops, moved, scratch=(), limit=12 << 20):
    return pl.pallas_call(
        kernel,
        out_shape=[
            pltpu.HBM(o[0], o[1]) if len(o) == 3 else jax.ShapeDtypeStruct(*o) for o in outs
        ],
        in_specs=specs,
        out_specs=out_specs,
        scratch_shapes=list(scratch),
        cost_estimate=pl.CostEstimate(flops=flops, bytes_accessed=moved, transcendentals=0),
        compiler_params=pltpu.CompilerParams(vmem_limit_bytes=limit),
    )


def hbm(x):
    return pltpu.with_memory_space_constraint(x, pltpu.HBM)


def pack(ids, gates, x, cot, wg, wu, wd):
    return call(
        pack_kernel,
        [((1152, 256), BF), ((2048, 256), BF), ((256, 128), BF), ((1, 128), F32)],
        [HBM] * 7,
        [VMEM, HBM, VMEM, VMEM],
        400000000,
        2600000,
        [
            pltpu.VMEM((1, 128), jnp.int32),
            pltpu.VMEM((128, 1024), BF),
            pltpu.VMEM((128, 1024), BF),
            pltpu.VMEM((2048, 256), BF),
            pltpu.SemaphoreType.DMA((9,)),
            pltpu.SemaphoreType.DMA((8,)),
        ],
    )(*map(hbm, (ids, gates, x, cot, wg, wu, wd)))


def expert_rows(index, recv, shards):
    return call(
        expert_kernel,
        [
            ((2048, 256), BF),
            ((1152, 256), BF, True),
            ((8, 256, 256), BF, True),
            ((3, 256, 256), BF, True),
            ((256, 384), BF, True),
        ],
        [SMEM] + [VMEM] * 5,
        [HBM] * 5,
        2000000000,
        6000000,
        [
            pltpu.VMEM((8, 256, 256), BF),
            pltpu.VMEM((2048, 256), BF),
            pltpu.VMEM((1152, 256), BF),
            pltpu.VMEM((8, 256, 256), BF),
            pltpu.VMEM((3, 256, 256), BF),
            pltpu.VMEM((256, 384), BF),
            pltpu.SemaphoreType.DMA((12,)),
        ],
        24 << 20,
    )(index, recv, *shards)


def other_grads(index, rows, slopes, hidden):
    return call(
        grads_kernel, [((1152, 256), BF)] * 3, [SMEM] + [VMEM] * 3, [VMEM] * 3, 450000000, 3000000
    )(index, rows, slopes, hidden)


def unpack_rows(recv, place, gates, cot):
    return call(
        unpack_kernel,
        [((128, 1024), BF), ((128, 1024), BF), ((1, 128), F32)],
        [VMEM] * 4,
        [VMEM] * 3,
        400000000,
        2000000,
        [pltpu.VMEM((256, 2048), BF)],
    )(recv, place, gates, cot)


def sum_grads(parts):
    return call(
        sum_kernel,
        [((1, 256, 384), BF), ((1, 256, 384), BF), ((1, 384, 256), BF)],
        [VMEM] * 4,
        [VMEM] * 3,
        0,
        3000000,
    )(*parts)


def per_device(x_rows, expert_ids, gates, cotangent, w_gate, w_up, w_down):
    groups = lax.axis_size("dp")

    def shift(value, k):
        return lax.ppermute(value, "dp", [(i, (i + k) % groups) for i in range(groups)])

    def exchange(rows):
        wire = rows.reshape(128, 16, 256)
        moved = lax.all_to_all(wire, "expert", split_axis=0, concat_axis=0, tiled=True)
        return moved.reshape(2048, 256)

    ids = expert_ids.reshape(1, 128)
    gate_row = gates.reshape(1, 128)
    own, send, place, gate_kept = pack(ids, gate_row, x_rows, cotangent, w_gate, w_up, w_down)
    shards = []
    for k in (1, 2, 3):
        shards.append(shift(own, k))
    recv = exchange(send)
    index = lax.axis_index("dp").astype(jnp.int32).reshape(1)
    out, g2, rows, slopes, hidden = expert_rows(index, recv, [own, *shards])
    returned = exchange(out)
    r2 = shift(g2, 2)
    g1, g3, g0 = other_grads(index, rows, slopes, hidden)
    r1 = shift(g1, 1)
    r3 = shift(g3, 3)
    parts = (g0, r1, r2, r3)
    gated_out, input_grad, gate_grad = unpack_rows(returned, place, gate_kept, cotangent)
    grads = sum_grads(parts)
    return (gated_out, input_grad, gate_grad.reshape(128, 1), *grads)


def solution(mesh):
    in_specs = (
        P(("dp", "expert"), None),
        P(("dp", "expert"), None),
        P(("dp", "expert"), None),
        P(("dp", "expert"), None),
        P("expert", "dp", None),
        P("expert", "dp", None),
        P("expert", None, "dp"),
    )
    out_specs = (
        P(("dp", "expert"), None),
        P(("dp", "expert"), None),
        P(("dp", "expert"), None),
        P("expert", "dp", None),
        P("expert", "dp", None),
        P("expert", None, "dp"),
    )
    return jax.shard_map(
        per_device, mesh=mesh, in_specs=in_specs, out_specs=out_specs, check_vma=False
    )
```
